32 devices in a mesh: section: 2 (over core), dp: 8 (over z, x), tensor: 2 (over y).
Axes of the slice: x: 2, y: 2, z: 4, core: 2. Of those that a mesh axis runs over, the one named last changes fastest.
Arguments:
- inputs: bfloat16 [4, 8, 256, 768], P(None, 'dp'), may hold values from -6 to 6
- segments: int32 [4, 8, 256], P(None, 'dp'), may hold values from 0 to 2, never falling along the last dimension, each value on 1 to 160 neighbouring positions
- cotangent: bfloat16 [4, 8, 256, 768], P(None, 'dp'), may hold values from -6 to 6
- norm_gain: bfloat16 [2, 768], P('section', 'dp'), may hold values from 0.5 to 1.5
- head_weight: bfloat16 [2, 768, 2, 1536], P('section', 'dp', None, 'tensor'), may hold values from -0.21875 to 0.21875
- step_weight: bfloat16 [2, 768, 24], P('section', 'dp', 'tensor'), may hold values from -0.21875 to 0.21875
- state_weight: bfloat16 [2, 768, 2, 128], P('section', 'dp'), may hold values from -0.21875 to 0.21875
- head_filter: float32 [2, 4, 1536], P('section', None, 'tensor'), may hold values from -3 to 3
- head_offset: float32 [2, 1536], P('section', 'tensor'), may hold values from -3 to 3
- state_filter: bfloat16 [2, 4, 2, 128], P('section', None, None, 'dp'), may hold values from -3 to 3
- state_offset: bfloat16 [2, 2, 128], P('section', None, 'dp'), may hold values from -3 to 3
- step_bias: float32 [2, 24], P('section', 'tensor'), may hold values from -5 to -1
- decay_log: float32 [2, 24], P('section', 'tensor'), may hold values from 0 to 2.77
- skip_scale: float32 [2, 24], P('section', 'tensor'), may hold values from 0.5 to 1.5
- gate_gain: float32 [2, 1536], P('section', 'tensor'), may hold values from 0.5 to 1.5
- output_weight: bfloat16 [2, 1536, 768], P('section', 'tensor', 'dp'), may hold values from -0.15625 to 0.15625
Outputs:
- layer_outputs: bfloat16 [2, 4, 8, 256, 768], P('section', None, 'dp', 'tensor')
- input_gradients: bfloat16 [2, 4, 8, 256, 768], P('section', None, 'dp', 'tensor')
- norm_gain_gradient: float32 [2, 768], P('section', 'dp')
- head_weight_gradient: float32 [2, 768, 2, 1536], P('section', 'dp', None, 'tensor')
- step_weight_gradient: float32 [2, 768, 24], P('section', 'dp', 'tensor')
- state_weight_gradient: float32 [2, 768, 2, 128], P('section', 'dp')
- head_filter_gradient: float32 [2, 4, 1536], P('section', None, 'tensor')
- head_offset_gradient: float32 [2, 1536], P('section', 'tensor')
- state_filter_gradient: float32 [2, 4, 2, 128], P('section', None, None, 'dp')
- state_offset_gradient: float32 [2, 2, 128], P('section', None, 'dp')
- step_bias_gradient: float32 [2, 24], P('section', 'tensor')
- decay_log_gradient: float32 [2, 24], P('section', 'tensor')
- skip_scale_gradient: float32 [2, 24], P('section', 'tensor')
- gate_gain_gradient: float32 [2, 1536], P('section', 'tensor')
- output_weight_gradient: float32 [2, 1536, 768], P('section', 'tensor', 'dp')
The draws below stay inside these ranges and needn't reach their ends.
Inputs may be any that keep to these rules, and one draw needn't show every extreme that they name: `segments`: along each sequence the segment numbers never fall, and every segment covers 1 to 160 tokens.
All inputs are finite; a program needn't handle non-finite values.
Results may differ from the reference program's by a relative error of at most 0.02.
Values may be sent and summed in bfloat16 or wider, within the bound.
No kernel may reach another device: no remote copies, remote signals or barrier semaphores. Data moves between devices by JAX's collectives and lax.ppermute only.
A program may use at most 192 MiB of HBM per device.

```python
import math
import jax
import jax.numpy as jnp
import numpy as np
from jax import lax

D = 768
INNER = 1536
HEADDIM = 64
STATE = 128
CONV = 4
NORM_GROUP = 192
LEN = 256
MICRO = 4
NHEADS = 24
SEQS = 8


def block_scale(key, extent, shards, least, high):
    level, own = 1.0, jax.random.fold_in(key, 6)
    for dim, blocks in shards:
        steps = jnp.exp(jax.random.uniform(jax.random.fold_in(own, dim), (blocks,), jnp.float32, least / len(shards), high / len(shards)))
        level = level * jnp.repeat(steps, extent[dim] // blocks).reshape([-1 if axis == dim else 1 for axis in range(len(extent))])
    return level


def length_profile(count, total, bound, slope):
    portions = [(1 << 20) // math.isqrt(rank ** slope) + 1 for rank in range(2, count + 1)]
    spare, counts = total - bound - (count - 1), [1] * (count - 1)
    while spare > 0:
        movable = [i for i in range(count - 1) if counts[i] < bound]
        mass, budget = sum([portions[i] for i in movable]), spare
        for i in movable:
            extra = min(bound - counts[i], max(1, budget * portions[i] // mass), spare)
            counts[i] = counts[i] + extra
            spare = spare - extra
    return np.array([bound] + counts)


def ragged(key, number_of, total, limit, skew):
    if number_of == 2:
        one = jax.random.randint(key, (), max(1, total - limit), min(limit, total - 1) + 1)
        return jnp.stack([one, total - one])
    lengths = jnp.asarray(length_profile(number_of, total, limit, skew), jnp.int32)
    pairs = (number_of - 1) // 2
    donor, sink = lengths[1:1 + 2 * pairs:2], lengths[2:2 + 2 * pairs:2]
    margin = jnp.minimum(donor - 1, limit - sink)
    passed = jax.random.randint(jax.random.fold_in(key, 1), (pairs,), 0, 1 << 20) % (margin + 1)
    lengths = lengths.at[1:1 + 2 * pairs:2].set(donor - passed).at[2:2 + 2 * pairs:2].set(sink + passed)
    return lengths[jax.random.permutation(jax.random.fold_in(key, 2), number_of)]


def scatter_about(rng, shape, scale, most, shards=(), kind=jnp.bfloat16):
    array = scale * jax.random.normal(rng, shape, jnp.float32)
    if shards:
        array = array * block_scale(rng, shape, shards, -0.22, 0.18)
    return jnp.clip(array, -most, most).astype(kind)


def setup_inputs(seed: int = 0) -> dict:
    keys = jax.random.split(jax.random.key(seed), 17)
    inputs = scatter_about(keys[0], (MICRO, SEQS, LEN, D), 1.0, 6.0, ((1, 8),))
    segments = jax.vmap(lambda own: jnp.searchsorted(jnp.cumsum(ragged(own, 3, LEN, LEN * 5 // 8, 0)), jnp.arange(LEN), side="right"))(jax.random.split(keys[1], MICRO * SEQS)).reshape((MICRO, SEQS, LEN)).astype(jnp.int32)
    cotangent = scatter_about(keys[2], (MICRO, SEQS, LEN, D), 1.0, 6.0, ((1, 8),))
    norm_gain = jnp.clip(1.0 + 0.1 * jax.random.normal(keys[3], (2, D), jnp.float32), 0.5, 1.5).astype(jnp.bfloat16)
    head_weight = scatter_about(keys[4], (2, D, 2, INNER), D ** -0.5, 0.21875, ((0, 2), (1, 8), (3, 2)))
    step_weight = scatter_about(keys[5], (2, D, NHEADS), D ** -0.5, 0.21875, ((0, 2), (1, 8), (2, 2)))
    state_weight = scatter_about(keys[6], (2, D, 2, STATE), D ** -0.5, 0.21875, ((0, 2), (1, 8)))
    head_filter = scatter_about(keys[7], (2, CONV, INNER), CONV ** -0.5, 3.0, ((0, 2), (2, 2)), jnp.float32)
    head_offset = scatter_about(keys[8], (2, INNER), 0.5, 3.0, ((0, 2), (1, 2)), jnp.float32)
    state_filter = scatter_about(keys[9], (2, CONV, 2, STATE), CONV ** -0.5, 3.0, ((0, 2), (3, 8)))
    state_offset = scatter_about(keys[10], (2, 2, STATE), 0.5, 3.0, ((0, 2), (2, 8)))
    step_bias = jnp.clip(-5.0 + 4.0 * jax.random.uniform(keys[11], (2, NHEADS), jnp.float32) ** block_scale(keys[11], (2, NHEADS), ((0, 2), (1, 2)), -0.2, 0.2), -5.0, -1.0)
    decay_log = jnp.clip(2.77 * jax.random.uniform(keys[12], (2, NHEADS), jnp.float32) ** block_scale(keys[12], (2, NHEADS), ((0, 2), (1, 2)), -0.2, 0.2), 0.0, 2.77)
    skip_scale = jnp.clip(0.5 + 1.0 * jax.random.uniform(keys[13], (2, NHEADS), jnp.float32) ** block_scale(keys[13], (2, NHEADS), ((0, 2), (1, 2)), -0.2, 0.2), 0.5, 1.5)
    gate_gain = jnp.clip(1.0 + 0.1 * jax.random.normal(keys[14], (2, INNER), jnp.float32), 0.5, 1.5)
    output_weight = scatter_about(keys[15], (2, INNER, D), INNER ** -0.5, 0.15625, ((0, 2), (1, 2), (2, 8)))
    return {"inputs": inputs, "segments": segments, "cotangent": cotangent, "norm_gain": norm_gain, "head_weight": head_weight, "step_weight": step_weight, "state_weight": state_weight, "head_filter": head_filter, "head_offset": head_offset, "state_filter": state_filter, "state_offset": state_offset, "step_bias": step_bias, "decay_log": decay_log, "skip_scale": skip_scale, "gate_gain": gate_gain, "output_weight": output_weight}


EPSILON = 1e-05

def causal_filter(values, filter_taps, offset, segment_row):
    length = values.shape[0]
    tap_count = filter_taps.shape[0]
    result = offset[None, :] + filter_taps[tap_count - 1][None, :] * values
    for lag_steps in range(1, tap_count):
        shifted = jnp.concatenate([jnp.zeros((lag_steps, values.shape[1]), values.dtype), values[:length - lag_steps]], 0)
        shifted_segment = jnp.concatenate([jnp.full((lag_steps,), -1, jnp.int32), segment_row[:length - lag_steps]], 0)
        same_segment = (shifted_segment == segment_row)[:, None]
        result = result + filter_taps[tap_count - 1 - lag_steps][None, :] * jnp.where(same_segment, shifted, 0.0)
    return result

def mixer_core(head_received, step_received, state_received, segment_row, head_filter, head_offset, state_filter, state_offset, step_bias, decay_log, skip_scale, gate_gain, head_size, group_size):
    length = head_received.shape[0]
    channels = head_received.shape[2]
    head_count = channels // head_size
    state_count = state_received.shape[2]
    gate_input = head_received[:, 0]
    mixer_input = jax.nn.silu(causal_filter(head_received[:, 1], head_filter, head_offset, segment_row))
    state_flat = jax.nn.silu(causal_filter(state_received.reshape(length, 2 * state_count), state_filter.reshape(state_filter.shape[0], 2 * state_count), state_offset.reshape(2 * state_count), segment_row))
    input_map = state_flat[:, :state_count]
    output_map = state_flat[:, state_count:]
    step_size = jax.nn.softplus(step_received + step_bias[None, :])
    decay_rate = -jnp.exp(decay_log)
    cumulative = jnp.cumsum(step_size * decay_rate[None, :], axis=0).T
    intersection = jnp.dot(output_map, input_map.T, precision=lax.Precision.HIGHEST)
    position = jnp.arange(length)
    allowed = (segment_row[:, None] == segment_row[None, :]) & (position[None, :] <= position[:, None])
    spread = jnp.minimum(cumulative[:, :, None] - cumulative[:, None, :], 0.0)
    weights = jnp.where(allowed[None], jnp.exp(spread), 0.0) * intersection[None] * step_size.T[:, None, :]
    per_head = mixer_input.reshape(length, head_count, head_size).transpose(1, 0, 2)
    scanned = jnp.einsum('hts,hsp->htp', weights, per_head, precision=lax.Precision.HIGHEST) + skip_scale[:, None, None] * per_head
    scanned = scanned.transpose(1, 0, 2).reshape(length, channels)
    gated_out = scanned * jax.nn.silu(gate_input)
    grouped = gated_out.reshape(length, channels // group_size, group_size)
    group_scale = lax.rsqrt(lax.optimization_barrier(jnp.mean(grouped * grouped, axis=-1, keepdims=True)) + EPSILON)
    return (grouped * group_scale).reshape(length, channels) * gate_gain[None, :]

def input_norm(rows, gain):
    return rows * lax.rsqrt(lax.optimization_barrier(jnp.mean(rows * rows, axis=-1, keepdims=True)) + EPSILON) * gain

def project(weights, rows):
    length = rows.shape[0]
    model_width = rows.shape[1]
    wide = rows.astype(jnp.float32)
    normalized_rows = input_norm(wide, weights[0].astype(jnp.float32)).astype(jnp.bfloat16)
    head_received = jnp.dot(normalized_rows, weights[1].reshape(model_width, -1), preferred_element_type=jnp.float32).reshape(length, 2, -1)
    step_received = jnp.dot(normalized_rows, weights[2], preferred_element_type=jnp.float32)
    state_received = jnp.dot(normalized_rows, weights[3].reshape(model_width, -1), preferred_element_type=jnp.float32).reshape(length, 2, -1)
    return (wide, normalized_rows, head_received, step_received, state_received)

def forward_sequence(weights, rows, segment_row):
    wide, normalized_rows, head_received, step_received, state_received = project(weights, rows)
    mixer_result = mixer_core(head_received, step_received, state_received, segment_row, *weights[4:12], HEADDIM, NORM_GROUP).astype(jnp.bfloat16)
    return (wide + jnp.dot(mixer_result, weights[12], preferred_element_type=jnp.float32)).astype(jnp.bfloat16)

def backward_sequence(weights, rows, segment_row, incoming_gradient):
    length = rows.shape[0]
    model_width = rows.shape[1]
    wide, normalized_rows, head_received, step_received, state_received = project(weights, rows)

    def core_map(head_arg, step_arg, state_arg, *small_params):
        return mixer_core(head_arg, step_arg, state_arg, segment_row, *small_params, HEADDIM, NORM_GROUP)
    mixer_result, core_back = jax.vjp(core_map, head_received, step_received, state_received, *weights[4:12])
    mixer_result_narrow = mixer_result.astype(jnp.bfloat16)
    output_term = jnp.dot(mixer_result_narrow.T, incoming_gradient, preferred_element_type=jnp.float32)
    mixed_tangent = jnp.dot(incoming_gradient, weights[12].T, preferred_element_type=jnp.float32)
    tangents = core_back(mixed_tangent)
    head_tangent_rows = tangents[0].astype(jnp.bfloat16).reshape(length, -1)
    step_tangent_rows = tangents[1].astype(jnp.bfloat16)
    state_tangent_rows = tangents[2].astype(jnp.bfloat16).reshape(length, -1)
    head_term = jnp.dot(normalized_rows.T, head_tangent_rows, preferred_element_type=jnp.float32).reshape(weights[1].shape)
    step_term = jnp.dot(normalized_rows.T, step_tangent_rows, preferred_element_type=jnp.float32)
    state_term = jnp.dot(normalized_rows.T, state_tangent_rows, preferred_element_type=jnp.float32).reshape(weights[3].shape)
    normed_tangent = jnp.dot(head_tangent_rows, weights[1].reshape(model_width, -1).T, preferred_element_type=jnp.float32)
    normed_tangent = normed_tangent + jnp.dot(step_tangent_rows, weights[2].T, preferred_element_type=jnp.float32)
    normed_tangent = normed_tangent + jnp.dot(state_tangent_rows, weights[3].reshape(model_width, -1).T, preferred_element_type=jnp.float32)
    unused_value, norm_back = jax.vjp(input_norm, wide, weights[0].astype(jnp.float32))
    wide_tangent, gain_term = norm_back(normed_tangent)
    result = (incoming_gradient.astype(jnp.float32) + wide_tangent).astype(jnp.bfloat16)
    return (result, (gain_term, head_term, step_term, state_term) + tuple(tangents[3:11]) + (output_term,))

def reference(inputs, segments, cotangent, norm_gain, head_weight, step_weight, state_weight, head_filter, head_offset, state_filter, state_offset, step_bias, decay_log, skip_scale, gate_gain, output_weight):
    total_rows = MICRO * SEQS
    rows_first = inputs.reshape(total_rows, LEN, D)
    segment_all = segments.reshape(total_rows, LEN)
    upstream_last = cotangent.reshape(total_rows, LEN, D)

    def layer_weights(layer):
        return (norm_gain[layer], head_weight[layer], step_weight[layer], state_weight[layer], head_filter[layer], head_offset[layer], state_filter[layer].astype(jnp.float32), state_offset[layer].astype(jnp.float32), step_bias[layer], decay_log[layer], skip_scale[layer], gate_gain[layer], output_weight[layer])

    def forward_layer(weights, rows_all):
        return lax.map(lambda pair: forward_sequence(weights, pair[0], pair[1]), (rows_all, segment_all))

    def backward_layer(weights, rows_all, upstream_all):
        zeros = tuple((jnp.zeros(weight.shape, jnp.float32) for weight in weights))

        def step_fn(carry, items):
            result, terms = backward_sequence(weights, items[0], items[1], items[2])
            return (tuple((total + term for total, term in zip(carry, terms))), result)
        totals, results = lax.scan(step_fn, zeros, (rows_all, segment_all, upstream_all))
        return (results, totals)
    first_weights = layer_weights(0)
    second_weights = layer_weights(1)
    rows_second = forward_layer(first_weights, rows_first)
    rows_third = forward_layer(second_weights, rows_second)
    tangent_second, totals_second = backward_layer(second_weights, rows_second, upstream_last)
    tangent_first, totals_first = backward_layer(first_weights, rows_first, tangent_second)
    shape_out = (2, MICRO, SEQS, LEN, D)
    layer_outputs = jnp.stack([rows_second, rows_third]).reshape(shape_out)
    input_gradients = jnp.stack([tangent_first, tangent_second]).reshape(shape_out)
    stacked = tuple((jnp.stack([first_total, second_total]) for first_total, second_total in zip(totals_first, totals_second)))
    return (layer_outputs, input_gradients, stacked[0], stacked[1], stacked[2], stacked[3], stacked[4], stacked[5], stacked[6], stacked[7], stacked[8], stacked[9], stacked[10], stacked[11], stacked[12])
```

```python
import functools

import jax
import jax.numpy as jnp
from jax import lax
from jax.experimental import pallas as pl
from jax.experimental.pallas import tpu as pltpu
from jax.sharding import PartitionSpec as P

HEADDIM = 64
NORM_GROUP = 192
EPSILON = 1e-05
LANES = 128

BF = jnp.bfloat16
F32 = jnp.float32


def mm(a, b):
    return lax.dot_general(a, b, (((1,), (0,)), ((), ())), preferred_element_type=F32)


def mm_nt(a, b):
    return lax.dot_general(a, b, (((1,), (1,)), ((), ())), preferred_element_type=F32)


def mm_tn(a, b):
    return lax.dot_general(a, b, (((0,), (0,)), ((), ())), preferred_element_type=F32)


def split(value, terms):
    parts = []
    for _ in range(terms - 1):
        high = value.astype(BF)
        parts.append(high)
        value = value - high.astype(F32)
    parts.append(value.astype(BF))
    return parts


def times_onehot(value, onehot, terms=2):
    total = None
    for part in split(value, terms):
        term = mm(part, onehot)
        total = term if total is None else total + term
    return total


def onehot_times(onehot, value, terms=3):
    total = None
    for part in split(value, terms):
        term = mm(onehot, part)
        total = term if total is None else total + term
    return total


def member(pair, width, transposed):
    shape = (LANES, LANES)
    channel = lax.broadcasted_iota(jnp.int32, shape, 1 if transposed else 0) + pair * LANES
    low = lax.broadcasted_iota(jnp.int32, shape, 0 if transposed else 1) * width
    inside = (channel >= low) & (channel < low + width)
    return jnp.where(inside, 1.0, 0.0).astype(BF)


def triangle(length, upper):
    row = lax.broadcasted_iota(jnp.int32, (length, length), 0)
    col = lax.broadcasted_iota(jnp.int32, (length, length), 1)
    return jnp.where(col >= row if upper else col <= row, 1.0, 0.0).astype(BF)


def sigmoid(value):
    return 0.5 * jnp.tanh(0.5 * value) + 0.5


def row_sum(value):
    return jnp.sum(value, axis=0, keepdims=True)


def filter_tile(value, taps, offset, masks):
    result = offset + taps[3] * value
    for lag in range(1, 4):
        result = result + taps[3 - lag] * (masks[lag - 1] * pltpu.roll(value, lag, 0))
    return result


def filter_tile_back(value, tangent, taps, masks):
    length = value.shape[0]
    back = taps[3] * tangent
    tap_terms = [None, None, None, row_sum(tangent * value)]
    for lag in range(1, 4):
        masked = masks[lag - 1] * tangent
        tap_terms[3 - lag] = row_sum(masked * pltpu.roll(value, lag, 0))
        back = back + taps[3 - lag] * pltpu.roll(masked, length - lag, 0)
    return back, tap_terms, row_sum(tangent)


def small_rows(wa, width, count, states):
    shard, each = width // count, states // count
    cols = wa[:, 2 * LANES : 3 * LANES]
    select = compact(width, shard, each, states, False)
    return cols.astype(F32).T, mm_tn(cols, select)


def compact(width, shard, each, states, transposed):
    shape = (states, width) if transposed else (width, states)
    row = lax.broadcasted_iota(jnp.int32, shape, 1 if transposed else 0)
    state = lax.broadcasted_iota(jnp.int32, shape, 0 if transposed else 1)
    shift = each.bit_length() - 1
    home = lax.shift_right_logical(state, shift) * shard + (state & (each - 1))
    return jnp.where(row == home, 1.0, 0.0).astype(BF)


def layer_kernel(plan, layer, scalars, *refs):
    backward, want_out, extra_u, extra_g, add_small, pairs, heads_real, count = plan
    refs = list(refs)
    take = lambda number: [refs.pop(0) for _ in range(number)]
    base_ref, seg_ref, hp_ref = take(3)
    extras_u = take(extra_u)
    blocks = take(4 * count)
    if backward:
        gbase_ref = take(1)[0]
        extras_g = take(extra_g)
        small_in = take(1)[0] if add_small else None
    out_ref = take(1)[0] if want_out else None
    mid_ref = take(1)[0] if extra_u else None
    if backward:
        ops_ref, du_ref, sm_ref = take(3)
    wa_ref, wb_ref, sems = take(3)
    (mask_s, z3, x3, f3, mx3, dtx3, y3, ga3, bc3, bcf3, xt3, hots, wide_hot, skip_s, cum_s, cum_t, grm, ss) = take(18)
    if backward:
        (w4, dm3, p4, dgs, dcum, ddt) = take(6)
    else:
        (mixed_s,) = take(1)
    length, width = base_ref.shape
    half = length // 2
    channels = pairs * LANES
    heads = 2 * pairs
    shard = width // count
    at_da = width
    at_dx = width + 3 * LANES + channels
    at_mixed = at_dx + channels
    at_g = at_mixed + channels

    def copies(home):
        jobs = []
        for hop in range(count):
            owner = scalars[1 + hop] if home else scalars[1 + count + hop]
            rows = pl.ds(pl.multiple_of(owner * shard, 16), shard)
            for which, target in ((0, wa_ref), (1, wb_ref)):
                source = blocks[(2 * which + (0 if home else 1)) * count + hop]
                jobs.append(
                    pltpu.make_async_copy(source, target.at[rows, :], sems.at[which, hop])
                )
        return jobs

    at_home = scalars[0] == layer

    @pl.when(at_home)
    def _():
        for job in copies(True):
            job.start()

    @pl.when(jnp.logical_not(at_home))
    def _():
        for job in copies(False):
            job.start()

    lane = lax.broadcasted_iota(jnp.int32, (length, LANES), 1)
    left = lane < HEADDIM

    def tile(ref, start, pair):
        return ref[start : start + 1, pl.ds(pl.multiple_of(pair * LANES, LANES), LANES)]

    def lanes_of(pair, base=0):
        return pl.ds(pl.multiple_of(base + pair * LANES, LANES), LANES)

    u = base_ref[...].astype(F32)
    if extra_u:
        for ref in extras_u:
            u = u + ref[...].astype(F32)
        narrow_u = u.astype(BF)
        mid_ref[...] = narrow_u
        u = narrow_u.astype(F32)
    inverse = lax.rsqrt(jnp.mean(u * u, axis=-1, keepdims=True) + EPSILON)
    seg_line = seg_ref[0:1, :]
    seg_cols = jnp.broadcast_to(seg_line, (LANES, length)).T
    row_id = lax.broadcasted_iota(jnp.int32, (length, LANES), 0)
    for lag in range(1, 4):
        same = (pltpu.roll(seg_cols, lag, 0) == seg_cols) & (row_id >= lag)
        mask_s[lag - 1] = jnp.where(same, 1.0, 0.0)
    masks = [mask_s[lag] for lag in range(3)]
    allowed = (jnp.concatenate([seg_cols] * (length // LANES), axis=1) == seg_line) & (
        lax.broadcasted_iota(jnp.int32, (length, length), 1)
        <= lax.broadcasted_iota(jnp.int32, (length, length), 0)
    )
    for pair in range(pairs):
        hots[0, pair] = member(pair, HEADDIM, False)
        hots[1, pair] = member(pair, HEADDIM, True)
        hots[2, pair] = member(pair, NORM_GROUP, False)
        hots[3, pair] = member(pair, NORM_GROUP, True)
        head_row = lax.broadcasted_iota(jnp.int32, (LANES, 2 * LANES), 0)
        head_lane = lax.broadcasted_iota(jnp.int32, (LANES, 2 * LANES), 1)
        wanted = 2 * pair + jnp.where(head_lane < LANES, 0, 1)
        wide_hot[pair] = jnp.where(head_row == wanted, 1.0, 0.0).astype(BF)
        skip_heads = jnp.broadcast_to(hp_ref[8:9, 0:LANES], (8, LANES))
        skip_s[:, pair * LANES : (pair + 1) * LANES] = times_onehot(
            skip_heads, member(pair, HEADDIM, True), 3
        )
    for job in copies(True):
        job.wait()

    gain_rows, state_rows = small_rows(wa_ref, width, count, LANES)
    gain = gain_rows[heads_real : heads_real + 1, :]
    first_row = heads_real + 1
    normed = (u * inverse * gain).astype(BF)
    if backward:
        ops_ref[:, 0:width] = normed
    small = mm(normed, wa_ref[:, 0 : 3 * LANES])
    zall = mm(normed, wa_ref[:, 3 * LANES :])
    xall = mm(normed, wb_ref[:, 0:channels])
    for pair in range(pairs):
        z3[pair] = zall[:, pair * LANES : (pair + 1) * LANES]
        x3[pair] = xall[:, pair * LANES : (pair + 1) * LANES]

    def state_taps(part):
        rows = [first_row + 2 * k + part for k in range(4)]
        return [state_rows[row : row + 1, :] for row in rows]

    narrow = []
    for part in range(2):
        pre = small[:, part * LANES : (part + 1) * LANES]
        bc3[part] = pre
        offset_row = first_row + 8 + part
        value = filter_tile(
            pre, state_taps(part), state_rows[offset_row : offset_row + 1, :], masks
        )
        bcf3[part] = value
        narrow.append((value * sigmoid(value)).astype(BF))
    input_map, output_map = narrow
    grm[...] = jnp.where(allowed, mm_nt(output_map, input_map), 0.0)

    real_head = lax.broadcasted_iota(jnp.int32, (1, LANES), 1) < heads_real
    step = small[:, 2 * LANES : 3 * LANES] + hp_ref[6:7, 0:LANES]
    rate = jnp.where(real_head, -jnp.exp(hp_ref[7:8, 0:LANES]), 0.0)
    dt = jnp.maximum(step, 0.0) + jnp.log1p(jnp.exp(-jnp.abs(step)))
    cum = onehot_times(triangle(length, False), dt * rate)
    cum_t[...] = cum.T
    for index, part in enumerate(split(cum, 3)):
        cum_s[index] = part

    def skip_of(pair):
        return tile(skip_s, 0, pair)

    ss[...] = jnp.zeros_like(ss)

    def forward_pair(pair, carry):
        masks = [mask_s[lag] for lag in range(3)]
        taps = [tile(hp_ref, k, pair) for k in range(4)]
        value = filter_tile(x3[pair], taps, tile(hp_ref, 4, pair), masks)
        f3[pair] = value
        mixer = value * sigmoid(value)
        mx3[pair] = mixer
        spread = times_onehot(dt, hots[1, pair])
        columns = sum(mm(cum_s[index], wide_hot[pair]) for index in range(3))
        dtx3[pair] = spread
        xt = (mixer * spread).astype(BF)
        xt3[pair] = xt
        scanned = jnp.zeros((length, LANES), F32)
        for side in range(2):
            head = 2 * pair + side
            column = columns[:, side * LANES : (side + 1) * LANES]
            line = cum_t[pl.ds(head, 1), :]
            masked = jnp.where(left if side == 0 else ~left, xt, jnp.zeros_like(xt))
            blocks = {}
            for bt, bs in ((0, 0), (1, 0), (1, 1)):
                rows = slice(bt * half, (bt + 1) * half)
                cols = slice(bs * half, (bs + 1) * half)
                fall = column[rows, 0:half] - line[:, cols]
                fade = jnp.exp(jnp.minimum(fall, 0.0) if bt == bs else fall)
                if backward:
                    p4[head, rows, cols] = fade.astype(BF)
                blocks[bt, bs] = (fade * grm[rows, cols]).astype(BF)
                if backward:
                    w4[head, rows, cols] = blocks[bt, bs]
            top = mm(blocks[0, 0], masked[0:half])
            low = mm(jnp.concatenate([blocks[1, 0], blocks[1, 1]], axis=1), masked)
            scanned = scanned + jnp.concatenate([top, low], axis=0)
        y3[pair] = scanned
        z = z3[pair]
        gated = (scanned + skip_of(pair) * mixer) * (z * sigmoid(z))
        ga3[pair] = gated
        ss[...] += times_onehot(gated * gated, hots[2, pair])
        return carry

    lax.fori_loop(0, pairs, forward_pair, 0)
    scale = lax.rsqrt(ss[...] * (1.0 / NORM_GROUP) + EPSILON)

    if not backward:

        def finish_pair(pair, carry):
            wide = times_onehot(scale, hots[3, pair])
            mixed_s[:, lanes_of(pair)] = (ga3[pair] * wide * tile(hp_ref, 5, pair)).astype(BF)
            return carry

        lax.fori_loop(0, pairs, finish_pair, 0)
        out_ref[...] = mm_nt(mixed_s[...], wb_ref[:, channels:]).astype(BF)
        return

    if extra_g:
        total = gbase_ref[...].astype(F32)
        for ref in extras_g:
            total = total + ref[...].astype(F32)
        upstream = total.astype(BF)
    else:
        upstream = gbase_ref[...]
    ops_ref[:, at_g : at_g + width] = upstream
    dmall = mm(upstream, wb_ref[:, channels:])

    sm_ref[...] = jnp.zeros_like(sm_ref)

    def put_small(row, span, value):
        if add_small:
            value = value + small_in[row : row + 1, span]
        sm_ref[row : row + 1, span] = value

    for pair in range(pairs):
        dm3[pair] = dmall[:, pair * LANES : (pair + 1) * LANES]
    ss[...] = jnp.zeros_like(ss)

    def norm_pair(pair, carry):
        wide = times_onehot(scale, hots[3, pair])
        gated = ga3[pair]
        gain = tile(hp_ref, 5, pair)
        unit = gated * wide
        ops_ref[:, lanes_of(pair, at_mixed)] = (unit * gain).astype(BF)
        tangent = dm3[pair]
        put_small(6, lanes_of(pair), row_sum(tangent * unit))
        tangent = tangent * gain
        dm3[pair] = tangent
        ss[...] += times_onehot(tangent * gated, hots[2, pair])
        return carry

    lax.fori_loop(0, pairs, norm_pair, 0)
    if want_out:
        out_ref[...] = mm_nt(ops_ref[:, at_mixed:at_g], wb_ref[:, channels:]).astype(BF)
    pull = scale * scale * scale * ss[...] * (1.0 / NORM_GROUP)
    dgs[...] = jnp.zeros_like(dgs)
    dcum[...] = jnp.zeros_like(dcum)
    ddt[...] = jnp.zeros_like(ddt)

    def back_pair(pair, carry):
        masks = [mask_s[lag] for lag in range(3)]
        spread_back = hots[3, pair]
        dgated = times_onehot(scale, spread_back) * dm3[pair] - ga3[pair] * times_onehot(
            pull, spread_back
        )
        z = z3[pair]
        zs = sigmoid(z)
        mixer = mx3[pair]
        scanned = y3[pair]
        skip = skip_of(pair)
        dy = dgated * (z * zs)
        dz = dgated * (scanned + skip * mixer) * (zs * (1.0 + z * (1.0 - zs)))
        ops_ref[:, lanes_of(pair, at_da + 3 * LANES)] = dz.astype(BF)
        put_small(5, lanes_of(pair), row_sum(dy * mixer))
        dyb = dy.astype(BF)
        xt = xt3[pair]
        sides = [jnp.where(left if side == 0 else ~left, dyb, jnp.zeros_like(dyb)) for side in (0, 1)]
        dxt = jnp.zeros((length, LANES), F32)
        for side in range(2):
            head, dys = 2 * pair + side, sides[side]
            top = mm_tn(w4[head, :, 0:half], dys)
            low = mm_tn(w4[head, half:length, half:length], dys[half:length])
            dxt = dxt + jnp.concatenate([top, low], axis=0)
        for bt, bs in ((0, 0), (1, 0), (1, 1)):
            rows = slice(bt * half, (bt + 1) * half)
            cols = slice(bs * half, (bs + 1) * half)
            dgs[rows, cols] += sum(
                mm_nt(sides[side][rows], xt[cols]) * p4[2 * pair + side, rows, cols].astype(F32)
                for side in range(2)
            )
        select = hots[0, pair]
        dcum[...] += times_onehot(dyb.astype(F32) * scanned - xt.astype(F32) * dxt, select)
        ddt[...] += times_onehot(mixer * dxt, select)
        value = f3[pair]
        vs = sigmoid(value)
        df = (dtx3[pair] * dxt + skip * dy) * (vs * (1.0 + value * (1.0 - vs)))
        taps = [tile(hp_ref, k, pair) for k in range(4)]
        dx, tap_terms, offset_term = filter_tile_back(x3[pair], df, taps, masks)
        ops_ref[:, lanes_of(pair, at_dx)] = dx.astype(BF)
        for k in range(4):
            put_small(k, lanes_of(pair), tap_terms[k])
        put_small(4, lanes_of(pair), offset_term)
        return carry

    lax.fori_loop(0, pairs, back_pair, 0)

    dgm = jnp.where(allowed, dgs[...], 0.0).astype(BF)
    tangents = [mm_tn(dgm, output_map), mm(dgm, input_map)]
    for part in range(2):
        span = slice(part * LANES, (part + 1) * LANES)
        value = bcf3[part]
        vs = sigmoid(value)
        df = tangents[part] * (vs * (1.0 + value * (1.0 - vs)))
        dv, tap_terms, offset_term = filter_tile_back(bc3[part], df, state_taps(part), masks)
        ops_ref[:, at_da + part * LANES : at_da + (part + 1) * LANES] = dv.astype(BF)
        for k in range(4):
            put_small(8 + 2 * k + part, slice(0, LANES), tap_terms[k])
        put_small(16 + part, slice(0, LANES), offset_term)

    dacc = onehot_times(triangle(length, True), dcum[...])
    dstep = (ddt[...] + rate * dacc) * sigmoid(step)
    ops_ref[:, at_da + 2 * LANES : at_da + 3 * LANES] = dstep.astype(BF)
    put_small(7, slice(0, LANES), row_sum(dstep))
    put_small(7, slice(LANES, 2 * LANES), row_sum(dt * dacc) * rate)

    dnorm = mm_nt(ops_ref[:, at_da:at_dx], wa_ref[...]) + mm_nt(
        ops_ref[:, at_dx:at_mixed], wb_ref[:, 0:channels]
    )
    put_small(18, slice(0, width), row_sum(dnorm * (u * inverse)))
    dg = dnorm * gain
    mean = jnp.mean(dg * u, axis=-1, keepdims=True)
    du_ref[...] = (inverse * dg - u * (inverse * inverse * inverse * mean)).astype(BF)


def whole_spec(shape):
    return pl.BlockSpec(shape, lambda i, s, n=len(shape): (0,) * n)


def run_layer(
    layer, backward, want_out, index, env, extras_u=(), extras_g=(), small_in=None
):
    inputs, cotangent, segs, hp, blocks, scalars, mine, heads_real = env
    length, width = inputs.shape[2:]
    local = inputs.shape[1]
    channels = hp.shape[-1]
    pairs = channels // LANES
    heads = 2 * pairs
    count = len(blocks) // 4

    def rows_spec():
        return pl.BlockSpec(
            (None, None, length, width),
            lambda i, s: (s[0] * mine + index // local, index % local, 0, 0),
        )

    any_spec = pl.BlockSpec(memory_space=pl.ANY)
    args = [inputs, segs, hp, *extras_u, *blocks]
    in_specs = [
        rows_spec(),
        pl.BlockSpec((None, 1, length), lambda i, s: (s[0] * mine * local + index, 0, 0)),
        pl.BlockSpec((None,) + hp.shape[1:], lambda i, s: (layer, 0, 0)),
    ]
    in_specs += [whole_spec((length, width)) for _ in extras_u]
    in_specs += [any_spec] * len(blocks)
    shapes = []
    if want_out:
        shapes.append(((length, width), BF))
    if extras_u:
        shapes.append(((length, width), BF))
    small_shape = (24, max(width, channels))
    if backward:
        args += [cotangent, *extras_g]
        in_specs += [rows_spec()] + [whole_spec((length, width)) for _ in extras_g]
        if small_in is not None:
            args.append(small_in)
            in_specs.append(whole_spec(small_shape))
        shapes += [
            ((length, 2 * width + 3 * LANES + 3 * channels), BF),
            ((length, width), BF),
            (small_shape, F32),
        ]
    tiles = (pairs, length, LANES)
    scratch = [
        pltpu.VMEM((width, 3 * LANES + channels), BF),
        pltpu.VMEM((width, 2 * channels), BF),
        pltpu.SemaphoreType.DMA((2, count)),
        pltpu.VMEM((3, length, LANES), F32),
    ]
    scratch += [pltpu.VMEM(tiles, F32) for _ in range(7)]
    scratch += [pltpu.VMEM((2, length, LANES), F32) for _ in range(2)]
    scratch += [
        pltpu.VMEM(tiles, BF),
        pltpu.VMEM((4, pairs, LANES, LANES), BF),
        pltpu.VMEM((pairs, LANES, 2 * LANES), BF),
        pltpu.VMEM((8, channels), F32),
        pltpu.VMEM((3, length, LANES), BF),
        pltpu.VMEM((LANES, length), F32),
        pltpu.VMEM((length, length), F32),
        pltpu.VMEM((length, LANES), F32),
    ]
    if backward:
        scratch += [
            pltpu.VMEM((heads, length, length), BF),
            pltpu.VMEM(tiles, F32),
            pltpu.VMEM((heads, length, length), BF),
            pltpu.VMEM((length, length), F32),
            pltpu.VMEM((length, LANES), F32),
            pltpu.VMEM((length, LANES), F32),
        ]
    else:
        scratch.append(pltpu.VMEM((length, channels), BF))
    passes = 3 if backward else 1
    cost = pl.CostEstimate(
        flops=passes * 2 * length * width * (3 * channels + 3 * LANES),
        bytes_accessed=passes * 2 * width * (3 * channels + 3 * LANES),
        transcendentals=passes * heads * length * length,
    )
    plan = (
        backward,
        want_out,
        len(extras_u),
        len(extras_g),
        small_in is not None,
        pairs,
        heads_real,
        count,
    )
    return pl.pallas_call(
        functools.partial(layer_kernel, plan, layer),
        grid_spec=pltpu.PrefetchScalarGridSpec(
            num_scalar_prefetch=1,
            grid=(1,),
            in_specs=in_specs,
            out_specs=[whole_spec(shape) for shape, _ in shapes],
            scratch_shapes=scratch,
        ),
        out_shape=[jax.ShapeDtypeStruct(s, d) for s, d in shapes],
        cost_estimate=cost,
        name=f"layer{layer}_{'back' if backward else 'front'}",
    )(scalars, *args)


def weight_kernel(number, count, heads_real, channels, scalars, *refs):
    refs = list(refs)
    take = lambda size: [refs.pop(0) for _ in range(size)]
    own, got, own_small, got_small = [], [], [], []
    for layer in range(2):
        own.append(take(number))
    for layer in range(2):
        got.append(take(number))
    for layer in range(2):
        own_small.append(take(1)[0])
    for layer in range(2):
        got_small.append(take(1)[0])
    sa_ref, sb_ref, hs_ref, buf, small, sems = take(6)
    width = sa_ref.shape[0] * sa_ref.shape[1]
    shard = sa_ref.shape[1]
    length = buf.shape[1]

    def copies(layer):
        jobs = []
        for i in range(number):
            jobs.append(pltpu.make_async_copy(own[layer][i], buf.at[i], sems.at[i]))
            jobs.append(
                pltpu.make_async_copy(got[layer][i], buf.at[number + i], sems.at[number + i])
            )
        jobs.append(pltpu.make_async_copy(own_small[layer], small.at[0], sems.at[2 * number]))
        jobs.append(pltpu.make_async_copy(got_small[layer], small.at[1], sems.at[2 * number + 1]))
        return jobs

    for layer in range(2):

        @pl.when(scalars[0] == layer)
        def _(layer=layer):
            for job in copies(layer):
                job.start()

    for job in copies(0):
        job.wait()
    at_da = width
    at_dx = width + 3 * LANES + channels
    at_mixed = at_dx + channels
    at_g = at_mixed + channels

    def piece(begin, end):
        return jnp.concatenate([buf[i, :, begin:end] for i in range(2 * number)], axis=0)

    def flipped(begin):
        return jnp.concatenate(
            [
                buf[i, :, begin : begin + width].astype(F32).T.astype(BF)
                for i in range(2 * number)
            ],
            axis=1,
        )

    def put(target, span, value):
        for owner in range(count):
            target[scalars[1 + 2 * count + owner], :, span] = value[
                owner * shard : (owner + 1) * shard
            ].astype(BF)

    totals = small[0] + small[1]
    hs_ref[...] = totals[0:8, 0:channels]
    normed = flipped(0)
    narrow = mm(normed, piece(at_da, at_da + 3 * LANES))
    expand = compact(width, shard, LANES // count, LANES, True)
    states = mm(totals[8:24, 0:LANES].astype(BF), expand)
    row = lax.broadcasted_iota(jnp.int32, (LANES, width), 0)
    sheet = jnp.where(row == heads_real, totals[18:19, 0:width], 0.0)
    for k in range(10):
        sheet = sheet + jnp.where(row == heads_real + 1 + k, states[k : k + 1, :], 0.0)
    put(sa_ref, slice(0, 2 * LANES), narrow[:, 0 : 2 * LANES])
    put(sa_ref, slice(2 * LANES, 3 * LANES), narrow[:, 2 * LANES :] + sheet.T)
    put(sa_ref, slice(3 * LANES, None), mm(normed, piece(at_da + 3 * LANES, at_dx)))
    put(sb_ref, slice(0, channels), mm(normed, piece(at_dx, at_mixed)))
    put(sb_ref, slice(channels, None), mm(flipped(at_g), piece(at_mixed, at_g)))


def run_weights(own, got, own_small, got_small, scalars, width, channels, heads_real, count):
    number = len(own[0])
    shard = width // count
    length, wide = own[0][0].shape
    args = [*own[0], *own[1], *got[0], *got[1], *own_small, *got_small]
    shapes = [
        ((count, shard, 3 * LANES + channels), BF),
        ((count, shard, 2 * channels), BF),
        ((8, channels), F32),
    ]
    cost = pl.CostEstimate(
        flops=4 * number * length * width * (3 * channels + 3 * LANES),
        bytes_accessed=4 * number * length * wide,
        transcendentals=0,
    )
    return pl.pallas_call(
        functools.partial(weight_kernel, number, count, heads_real, channels),
        grid_spec=pltpu.PrefetchScalarGridSpec(
            num_scalar_prefetch=1,
            grid=(1,),
            in_specs=[pl.BlockSpec(memory_space=pl.ANY)] * len(args),
            out_specs=[whole_spec(shape) for shape, _ in shapes],
            scratch_shapes=[
                pltpu.VMEM((2 * number, length, wide), BF),
                pltpu.VMEM((2,) + own_small[0].shape, F32),
                pltpu.SemaphoreType.DMA((2 * number + 2,)),
            ],
        ),
        out_shape=[jax.ShapeDtypeStruct(s, d) for s, d in shapes],
        cost_estimate=cost,
        name="weight_terms",
    )(scalars, *args)


def pack_kernel(channels_real, state_ref, spare_ref, head_ref, out_ref, a_ref, b_ref):
    shard = state_ref.shape[0]
    channels = b_ref.shape[1] // 2
    a_ref[:, 0 : 2 * LANES] = state_ref[...]
    a_ref[:, 2 * LANES : 3 * LANES] = spare_ref[...]
    row = lax.broadcasted_iota(jnp.int32, (shard, shard), 0)
    col = lax.broadcasted_iota(jnp.int32, (shard, shard), 1)
    identity = jnp.where(row == col, 1.0, 0.0).astype(BF)
    if channels != channels_real:
        a_ref[:, 3 * LANES :] = jnp.zeros((shard, channels), BF)
        b_ref[...] = jnp.zeros_like(b_ref)
    a_ref[:, 3 * LANES : 3 * LANES + channels_real] = head_ref[:, 0, :]
    b_ref[:, 0:channels_real] = head_ref[:, 1, :]
    b_ref[:, channels : channels + channels_real] = mm_nt(identity, out_ref[...]).astype(BF)


def run_pack(state, spare, head, out, channels):
    shard = state.shape[0]
    shapes = [(shard, 3 * LANES + channels), (shard, 2 * channels)]
    return pl.pallas_call(
        functools.partial(pack_kernel, head.shape[2]),
        out_shape=[jax.ShapeDtypeStruct(shape, BF) for shape in shapes],
        name="pack",
    )(state, spare, head, out)


def ring_order(count):
    return [i for i in range(0, count, 2)] + [i for i in range(1, count, 2)][::-1]


def swap(value, axis):
    return lax.ppermute(value, axis, [(0, 1), (1, 0)])


def on_device(
    inputs,
    segments,
    cotangent,
    norm_gain,
    head_weight,
    step_weight,
    state_weight,
    head_filter,
    head_offset,
    state_filter,
    state_offset,
    step_bias,
    decay_log,
    skip_scale,
    gate_gain,
    output_weight,
):
    sections = lax.axis_size("section")
    count = lax.axis_size("dp")
    tensors = lax.axis_size("tensor")
    section = lax.axis_index("section")
    dp = lax.axis_index("dp")
    tensor = lax.axis_index("tensor")
    first = section == 0
    micros, local, length, width = inputs.shape
    mine = micros // sections
    number = mine * local
    share_rows = length // tensors
    share_start = tensor * share_rows
    shard = width // count
    channels_real = head_filter.shape[2]
    heads_real = step_bias.shape[1]
    states = state_weight.shape[3]
    pairs = -(-heads_real // 2)
    channels = pairs * LANES
    pad_channels = channels - channels_real

    def pad_last(value, size):
        extra = size - value.shape[-1]
        if extra == 0:
            return value
        return jnp.pad(value, [(0, 0)] * (value.ndim - 1) + [(0, extra)])

    lanes_each = states // count
    tiny = jnp.concatenate([state_filter[0].reshape(8, lanes_each), state_offset[0]], axis=0).T
    tiny = jnp.pad(tiny, ((0, shard - lanes_each), (0, 0)))
    spare = pad_last(
        jnp.concatenate([step_weight[0], norm_gain[0][:, None], tiny], axis=1), LANES
    )
    block_a, block_b = run_pack(
        state_weight[0].reshape(shard, 2 * states), spare, head_weight[0], output_weight[0], channels
    )

    order = ring_order(count)
    where_is = [order.index(i) for i in range(count)]
    order_table = jnp.array(order, jnp.int32)
    position = jnp.array(where_is, jnp.int32)[dp]
    heading = jnp.where(first, 1, -1)
    hops = []
    for i in range(count):
        hops.append((order[i], order[(i + 1) % count]))
        hops.append((count + order[i], count + order[(i - 1) % count]))

    def around(value):
        return lax.ppermute(value, ("section", "dp"), hops)

    def block_at(offset):
        return order_table[(position + offset) % count]

    def gather(block):
        own, other = [], []
        current = block
        for hop in range(count):
            if hop:
                current = around(current)
            own.append(current)
            other.append(swap(current, "section"))
        return own + other

    blocks = gather(block_a) + gather(block_b)
    hop_list = jnp.arange(count)
    ring_slot = ((position - jnp.array(where_is, jnp.int32)) * heading - 1) % count
    scalars = jnp.concatenate(
        [
            section[None],
            order_table[(position - heading * hop_list) % count],
            order_table[(position + heading * hop_list) % count],
            ring_slot,
        ]
    ).astype(jnp.int32)

    lines = [pad_last(value, channels) for value in (step_bias, decay_log, skip_scale)]
    wide = [pad_last(value, channels) for value in (head_filter[0], head_offset, gate_gain)]
    own_params = jnp.concatenate(wide + lines, axis=0)
    other_params = swap(own_params, "section")
    hp = jnp.stack(
        [
            jnp.where(first, own_params, other_params),
            jnp.where(first, other_params, own_params),
        ]
    )

    segs = segments.reshape(micros * local, 1, length).astype(F32)
    env = (inputs, cotangent, segs, hp, blocks, scalars, mine, heads_real)

    def pieces(partial):
        if tensors == 2:
            return (partial, swap(partial, "tensor"))
        return (lax.psum(partial.astype(F32), "tensor"),)

    def share_of(value):
        return lax.dynamic_slice_in_dim(value, share_start, share_rows, 0)

    def combine_share(base, partial):
        if tensors == 2:
            sent = lax.dynamic_slice_in_dim(partial, (1 - tensor) * share_rows, share_rows, 0)
            total = share_of(partial).astype(F32) + swap(sent, "tensor").astype(F32)
        else:
            total = lax.psum_scatter(
                partial.astype(F32), "tensor", scatter_dimension=0, tiled=True
            )
        return (share_of(base).astype(F32) + total).astype(BF)

    def place(zero, one):
        zero, one = jnp.stack(zero), jnp.stack(one)
        kept = jnp.where(first, zero, one)
        got = swap(jnp.where(first, one, zero), "section")
        early = jnp.where(first, kept, got)
        late = jnp.where(first, got, kept)
        joined = jnp.concatenate([early, late], axis=0)
        return joined.reshape(1, micros, local, share_rows, width)

    to_one = lambda value: lax.ppermute(value, "section", [(0, 1)])
    to_zero = lambda value: lax.ppermute(value, "section", [(1, 0)])

    fronts = [pieces(run_layer(0, False, True, i, env)[0]) for i in range(number)]
    middle, outs, backs, ops_one, got_one = [], [], [], [], []
    small_one = None
    for i in range(number):
        partial, rows, ops, back, small_one = run_layer(
            1, True, True, i, env, extras_u=fronts[i], small_in=small_one
        )
        middle.append(rows)
        backs.append(pieces(back))
        outs.append(partial)
        ops_one.append(ops)
        got_one.append(to_one(ops))
    got_small_one = to_one(small_one)
    ops_zero, got_zero, front_backs = [], [], []
    small_zero = None
    for i in range(number):
        ops, back, small_zero = run_layer(
            0, True, False, i, env, extras_g=backs[i], small_in=small_zero
        )
        ops_zero.append(ops)
        got_zero.append(to_zero(ops))
        front_backs.append(back)
    got_small_zero = to_zero(small_zero)

    sums_a, sums_b, head_small = run_weights(
        (ops_zero, ops_one),
        (got_zero, got_one),
        (small_zero, small_one),
        (got_small_zero, got_small_one),
        scalars,
        width,
        channels,
        heads_real,
        count,
    )

    heads_total = head_small
    doubling = count & (count - 1) == 0
    if not doubling:
        heads_total = lax.psum(heads_total, "dp")
    mid_rows = [ops[:, ops.shape[1] - width :] for ops in ops_zero]
    last, front_grads, outputs, input_grads = None, None, None, None
    total_a, total_b = sums_a[0], sums_b[0]
    bit = 1
    for hop in range(1, count):
        total_a = around(total_a).astype(F32) + sums_a[hop].astype(F32)
        total_b = around(total_b).astype(F32) + sums_b[hop].astype(F32)
        if hop < count - 1:
            total_a, total_b = total_a.astype(BF), total_b.astype(BF)
        if hop >= 2 and bit < count and doubling:
            total_b, heads_total = lax.optimization_barrier((total_b, heads_total))
            heads_total = heads_total + lax.ppermute(
                heads_total, "dp", [(i, i ^ bit) for i in range(count)]
            )
            bit *= 2
        if hop == 1:
            total_a, outs = lax.optimization_barrier((total_a, outs))
            last = [combine_share(rows, partial) for rows, partial in zip(middle, outs)]
        if hop == 2:
            total_a, front_backs = lax.optimization_barrier((total_a, front_backs))
            front_grads = [combine_share(rows, back) for rows, back in zip(mid_rows, front_backs)]
        if hop == 3:
            total_a, last = lax.optimization_barrier((total_a, last))
            outputs = place([share_of(value) for value in middle], last)
        if hop == 4:
            total_a, front_grads = lax.optimization_barrier((total_a, front_grads))
            input_grads = place(front_grads, [share_of(value) for value in mid_rows])
    shared = total_a[:, : 2 * states + LANES]
    if tensors == 2:
        shared_sum = shared + swap(shared.astype(BF), "tensor").astype(F32)
    else:
        shared_sum = lax.psum(shared.astype(BF), "tensor").astype(F32)
    state_grad = shared_sum[:, : 2 * states].reshape(shard, 2, states)
    step_grad = shared[:, 2 * states : 2 * states + heads_real]
    spare_sum = shared_sum[:, 2 * states + heads_real :]
    gain_grad = spare_sum[:, 0]
    tiny_sum = spare_sum[:lanes_each, 1:11].T
    filter_grad = tiny_sum[0:8].reshape(4, 2, lanes_each)
    offset_grad = tiny_sum[8:10]
    head_grad = jnp.stack(
        [total_a[:, 2 * states + LANES :][:, :channels_real], total_b[:, :channels_real]], axis=1
    )
    output_grad = total_b[:, channels : channels + channels_real].T

    skip_grad = heads_total[5].reshape(-1, HEADDIM).sum(axis=1)[:heads_real]

    return (
        outputs,
        input_grads,
        gain_grad[None],
        head_grad[None],
        step_grad[None],
        state_grad[None],
        heads_total[None, 0:4, :channels_real],
        heads_total[None, 4, :channels_real],
        filter_grad[None],
        offset_grad[None],
        heads_total[None, 7, 0:heads_real],
        heads_total[None, 7, LANES : LANES + heads_real],
        skip_grad[None],
        heads_total[None, 6, :channels_real],
        output_grad[None],
    )


def solution(mesh):
    placed = (
        P(None, "dp", None, None),
        P(None, "dp", None),
        P(None, "dp", None, None),
        P("section", "dp"),
        P("section", "dp", None, "tensor"),
        P("section", "dp", "tensor"),
        P("section", "dp", None, None),
        P("section", None, "tensor"),
        P("section", "tensor"),
        P("section", None, None, "dp"),
        P("section", None, "dp"),
        P("section", "tensor"),
        P("section", "tensor"),
        P("section", "tensor"),
        P("section", "tensor"),
        P("section", "tensor", "dp"),
    )
    return jax.shard_map(
        on_device,
        mesh=mesh,
        in_specs=placed,
        out_specs=(
            P("section", None, "dp", "tensor", None),
            P("section", None, "dp", "tensor", None),
            P("section", "dp"),
            P("section", "dp", None, "tensor"),
            P("section", "dp", "tensor"),
            P("section", "dp", None, None),
            P("section", None, "tensor"),
            P("section", "tensor"),
            P("section", None, None, "dp"),
            P("section", None, "dp"),
            P("section", "tensor"),
            P("section", "tensor"),
            P("section", "tensor"),
            P("section", "tensor"),
            P("section", "tensor", "dp"),
        ),
        check_vma=False,
    )
```

```python
import functools

import jax
import jax.numpy as jnp
from jax import lax
from jax.experimental import pallas as pl
from jax.experimental.pallas import tpu as pltpu
from jax.sharding import PartitionSpec as P


HEADDIM = 64
NORM_GROUP = 192
EPSILON = 1e-05
LANES = 128
SMALL = 32

BF = jnp.bfloat16
F32 = jnp.float32


def mm(a, b):
    return lax.dot_general(a, b, (((1,), (0,)), ((), ())), preferred_element_type=F32)


def mm_nt(a, b):
    return lax.dot_general(a, b, (((1,), (1,)), ((), ())), preferred_element_type=F32)


def mm_tn(a, b):
    return lax.dot_general(a, b, (((0,), (0,)), ((), ())), preferred_element_type=F32)


def split(value, terms):
    parts = []
    for _ in range(terms - 1):
        high = value.astype(BF)
        parts.append(high)
        value = value - high.astype(F32)
    parts.append(value.astype(BF))
    return parts


def times_onehot(value, onehot, terms=2):
    total = None
    for part in split(value, terms):
        term = mm(part, onehot)
        total = term if total is None else total + term
    return total


def halves(value):
    return jnp.concatenate(split(value, 2), axis=1)


def twice(onehot):
    return jnp.concatenate([onehot, onehot], axis=0)


def onehot_times(onehot, value, terms=3):
    total = None
    for part in split(value, terms):
        term = mm(onehot, part)
        total = term if total is None else total + term
    return total


def member(pair, width, transposed):
    shape = (LANES, LANES)
    channel = lax.broadcasted_iota(jnp.int32, shape, 1 if transposed else 0) + pair * LANES
    low = lax.broadcasted_iota(jnp.int32, shape, 0 if transposed else 1) * width
    inside = (channel >= low) & (channel < low + width)
    return jnp.where(inside, 1.0, 0.0).astype(BF)


def triangle(length, upper):
    row = lax.broadcasted_iota(jnp.int32, (length, length), 0)
    col = lax.broadcasted_iota(jnp.int32, (length, length), 1)
    return jnp.where(col >= row if upper else col <= row, 1.0, 0.0).astype(BF)


def sigmoid(value):
    return 0.5 * jnp.tanh(0.5 * value) + 0.5


def row_sum(value):
    return jnp.sum(value, axis=0, keepdims=True)


def filter_tile(value, taps, offset, masks):
    result = offset + taps[3] * value
    for lag in range(1, 4):
        result = result + taps[3 - lag] * (masks[lag - 1] * pltpu.roll(value, lag, 0))
    return result


def filter_tile_back(value, tangent, taps, masks):
    length = value.shape[0]
    back = taps[3] * tangent
    tap_terms = [None, None, None, row_sum(tangent * value)]
    for lag in range(1, 4):
        ahead = pltpu.roll(masks[lag - 1] * tangent, length - lag, 0)
        tap_terms[3 - lag] = row_sum(ahead * value)
        back = back + taps[3 - lag] * ahead
    return back, tap_terms, row_sum(tangent)


def small_rows(wa, width, count, states):
    shard, each = width // count, states // count
    cols = wa[:, 2 * LANES : 3 * LANES]
    select = compact(width, shard, each, states, False)
    return cols.astype(F32).T, mm_tn(cols, select)


def compact(width, shard, each, states, transposed):
    shape = (states, width) if transposed else (width, states)
    row = lax.broadcasted_iota(jnp.int32, shape, 1 if transposed else 0)
    state = lax.broadcasted_iota(jnp.int32, shape, 0 if transposed else 1)
    shift = each.bit_length() - 1
    home = lax.shift_right_logical(state, shift) * shard + (state & (each - 1))
    return jnp.where(row == home, 1.0, 0.0).astype(BF)


def layer_kernel(plan, layer, scalars, *refs):
    backward, want_out, extra_u, extra_g, pairs, heads_real, count = plan
    refs = list(refs)
    take = lambda number: [refs.pop(0) for _ in range(number)]
    base_ref, seg_ref, hp_ref = take(3)
    extras_u = take(extra_u)
    blocks = take(4 * count)
    if backward:
        gbase_ref = take(1)[0]
        extras_g = take(extra_g)
    out_ref = take(1)[0] if want_out else None
    mid_ref = take(1)[0] if extra_u else None
    if backward:
        ops_ref, du_ref = take(2)
        gmid_ref = take(1)[0] if extra_g else None
    wa_ref, wb_ref, sems = take(3)
    (mask_s, z3, x3, f3, mx3, dtx3, y3, ga3, bc3, bcf3, xt3, hots, wide_hot, skip_s, dt_s, scale_s, pull_s, cum_s, cum_t, grm, ss) = take(21)
    if backward:
        (w4, dm3, p4, dgs, dcum, ddt, sm_ref) = take(7)
    else:
        (mixed_s,) = take(1)
    length, width = base_ref.shape
    half = length // 2
    channels = pairs * LANES
    shard = width // count
    at_da = width
    at_dx = width + 3 * LANES + channels
    at_mixed = at_dx + channels
    at_g = at_mixed + channels

    def copies(home):
        jobs = []
        for hop in range(count):
            owner = scalars[1 + hop] if home else scalars[1 + count + hop]
            rows = pl.ds(pl.multiple_of(owner * shard, 16), shard)
            for which, target in ((0, wa_ref), (1, wb_ref)):
                source = blocks[(2 * which + (0 if home else 1)) * count + hop]
                jobs.append(
                    pltpu.make_async_copy(source, target.at[rows, :], sems.at[which, hop])
                )
        return jobs

    at_home = scalars[0] == layer

    @pl.when(at_home)
    def _():
        for job in copies(True):
            job.start()

    @pl.when(jnp.logical_not(at_home))
    def _():
        for job in copies(False):
            job.start()

    lane = lax.broadcasted_iota(jnp.int32, (length, LANES), 1)
    left = lane < HEADDIM

    def tile(ref, start, pair):
        return ref[start : start + 1, pl.ds(pl.multiple_of(pair * LANES, LANES), LANES)]

    def lanes_of(pair, base=0):
        return pl.ds(pl.multiple_of(base + pair * LANES, LANES), LANES)

    u = base_ref[...].astype(F32)
    if extra_u:
        for ref in extras_u:
            u = u + ref[...].astype(F32)
        narrow_u = u.astype(BF)
        mid_ref[...] = narrow_u
        u = narrow_u.astype(F32)
    inverse = lax.rsqrt(jnp.mean(u * u, axis=-1, keepdims=True) + EPSILON)
    seg_line = seg_ref[0:1, :]
    seg_cols = jnp.broadcast_to(seg_line, (LANES, length)).T
    row_id = lax.broadcasted_iota(jnp.int32, (length, LANES), 0)
    for lag in range(1, 4):
        same = (pltpu.roll(seg_cols, lag, 0) == seg_cols) & (row_id >= lag)
        mask_s[lag - 1] = jnp.where(same, 1.0, 0.0)
    masks = [mask_s[lag] for lag in range(3)]
    allowed = (jnp.concatenate([seg_cols] * (length // LANES), axis=1) == seg_line) & (
        lax.broadcasted_iota(jnp.int32, (length, length), 1)
        <= lax.broadcasted_iota(jnp.int32, (length, length), 0)
    )
    for pair in range(pairs):
        hots[0, pair] = twice(member(pair, HEADDIM, False))
        hots[1, pair] = twice(member(pair, HEADDIM, True))
        hots[2, pair] = twice(member(pair, NORM_GROUP, False))
        hots[3, pair] = twice(member(pair, NORM_GROUP, True))
        head_row = lax.broadcasted_iota(jnp.int32, (LANES, 2 * LANES), 0)
        head_lane = lax.broadcasted_iota(jnp.int32, (LANES, 2 * LANES), 1)
        wanted = 2 * pair + jnp.where(head_lane < LANES, 0, 1)
        one_wide = jnp.where(head_row == wanted, 1.0, 0.0).astype(BF)
        wide_hot[pair] = jnp.concatenate([one_wide] * 3, axis=0)
        skip_heads = jnp.broadcast_to(hp_ref[8:9, 0:LANES], (8, LANES))
        skip_s[:, pair * LANES : (pair + 1) * LANES] = times_onehot(
            skip_heads, member(pair, HEADDIM, True), 3
        )
    for job in copies(True):
        job.wait()

    gain_rows, state_rows = small_rows(wa_ref, width, count, LANES)
    gain = gain_rows[heads_real : heads_real + 1, :]
    first_row = heads_real + 1
    normed = (u * inverse * gain).astype(BF)
    if backward:
        ops_ref[0:length, 0:width] = normed
    small = mm(normed, wa_ref[:, 0 : 3 * LANES])
    zall = mm(normed, wa_ref[:, 3 * LANES :])
    xall = mm(normed, wb_ref[:, 0:channels])
    for pair in range(pairs):
        z3[pair] = zall[:, pair * LANES : (pair + 1) * LANES]
        x3[pair] = xall[:, pair * LANES : (pair + 1) * LANES]

    def state_taps(part):
        rows = [first_row + 2 * k + part for k in range(4)]
        return [state_rows[row : row + 1, :] for row in rows]

    narrow = []
    for part in range(2):
        pre = small[:, part * LANES : (part + 1) * LANES]
        bc3[part] = pre
        offset_row = first_row + 8 + part
        value = filter_tile(
            pre, state_taps(part), state_rows[offset_row : offset_row + 1, :], masks
        )
        bcf3[part] = value
        narrow.append((value * sigmoid(value)).astype(BF))
    input_map, output_map = narrow
    grm[...] = jnp.where(allowed, mm_nt(output_map, input_map), 0.0)

    real_head = lax.broadcasted_iota(jnp.int32, (1, LANES), 1) < heads_real
    step = small[:, 2 * LANES : 3 * LANES] + hp_ref[6:7, 0:LANES]
    rate = jnp.where(real_head, -jnp.exp(hp_ref[7:8, 0:LANES]), 0.0)
    dt = jnp.maximum(step, 0.0) + jnp.log1p(jnp.exp(-jnp.abs(step)))
    cum = onehot_times(triangle(length, False), dt * rate)
    cum_t[...] = cum.T
    cum_s[...] = jnp.concatenate(split(cum, 3), axis=1)
    dt_s[...] = halves(dt)

    def skip_of(pair):
        return tile(skip_s, 0, pair)

    ss[...] = jnp.zeros_like(ss)

    def forward_pair(pair, carry):
        masks = [mask_s[lag] for lag in range(3)]
        taps = [tile(hp_ref, k, pair) for k in range(4)]
        value = filter_tile(x3[pair], taps, tile(hp_ref, 4, pair), masks)
        f3[pair] = value
        mixer = value * sigmoid(value)
        mx3[pair] = mixer
        spread = mm(dt_s[...], hots[1, pair])
        columns = mm(cum_s[...], wide_hot[pair])
        dtx3[pair] = spread
        xt = (mixer * spread).astype(BF)
        xt3[pair] = xt
        scanned = jnp.zeros((length, LANES), F32)
        for side in range(2):
            head = 2 * pair + side
            column = columns[:, side * LANES : (side + 1) * LANES]
            line = cum_t[pl.ds(head, 1), :]
            masked = jnp.where(left if side == 0 else ~left, xt, jnp.zeros_like(xt))
            blocks = {}
            for bt, bs in ((0, 0), (1, 0), (1, 1)):
                rows = slice(bt * half, (bt + 1) * half)
                cols = slice(bs * half, (bs + 1) * half)
                fall = column[rows, 0:half] - line[:, cols]
                fade = jnp.exp(jnp.minimum(fall, 0.0) if bt == bs else fall)
                if backward:
                    p4[head, rows, cols] = fade.astype(BF)
                blocks[bt, bs] = (fade * grm[rows, cols]).astype(BF)
                if backward:
                    w4[head, rows, cols] = blocks[bt, bs]
            top = mm(blocks[0, 0], masked[0:half])
            low = mm(jnp.concatenate([blocks[1, 0], blocks[1, 1]], axis=1), masked)
            scanned = scanned + jnp.concatenate([top, low], axis=0)
        y3[pair] = scanned
        z = z3[pair]
        gated = (scanned + skip_of(pair) * mixer) * (z * sigmoid(z))
        ga3[pair] = gated
        ss[...] += mm(halves(gated * gated), hots[2, pair])
        return carry

    lax.fori_loop(0, pairs, forward_pair, 0, unroll=2)
    scale = lax.rsqrt(ss[...] * (1.0 / NORM_GROUP) + EPSILON)
    scale_s[...] = halves(scale)

    if not backward:

        def finish_pair(pair, carry):
            wide = mm(scale_s[...], hots[3, pair])
            mixed_s[:, lanes_of(pair)] = (ga3[pair] * wide * tile(hp_ref, 5, pair)).astype(BF)
            return carry

        lax.fori_loop(0, pairs, finish_pair, 0)
        out_ref[...] = mm_nt(mixed_s[...], wb_ref[:, channels:]).astype(BF)
        return

    if extra_g:
        total = gbase_ref[...].astype(F32)
        for ref in extras_g:
            total = total + ref[...].astype(F32)
        upstream = total.astype(BF)
        gmid_ref[...] = upstream
    else:
        upstream = gbase_ref[...]
    ops_ref[0:length, at_g : at_g + width] = upstream
    dmall = mm(upstream, wb_ref[:, channels:])

    sm_ref[...] = jnp.zeros_like(sm_ref)

    def put_small(row, span, value):
        sm_ref[row : row + 1, span] = value

    for pair in range(pairs):
        dm3[pair] = dmall[:, pair * LANES : (pair + 1) * LANES]
    ss[...] = jnp.zeros_like(ss)

    def norm_pair(pair, carry):
        wide = mm(scale_s[...], hots[3, pair])
        gated = ga3[pair]
        gain = tile(hp_ref, 5, pair)
        unit = gated * wide
        ops_ref[0:length, lanes_of(pair, at_mixed)] = (unit * gain).astype(BF)
        tangent = dm3[pair]
        put_small(6, lanes_of(pair), row_sum(tangent * unit))
        tangent = tangent * gain
        dm3[pair] = tangent
        ss[...] += mm(halves(tangent * gated), hots[2, pair])
        return carry

    lax.fori_loop(0, pairs, norm_pair, 0, unroll=2)
    if want_out:
        out_ref[...] = mm_nt(ops_ref[0:length, at_mixed:at_g], wb_ref[:, channels:]).astype(BF)
    pull_s[...] = halves(scale * scale * scale * ss[...] * (1.0 / NORM_GROUP))
    dgs[...] = jnp.zeros_like(dgs)
    dcum[...] = jnp.zeros_like(dcum)
    ddt[...] = jnp.zeros_like(ddt)

    def back_pair(pair, carry):
        masks = [mask_s[lag] for lag in range(3)]
        spread_back = hots[3, pair]
        dgated = mm(scale_s[...], spread_back) * dm3[pair] - ga3[pair] * mm(
            pull_s[...], spread_back
        )
        z = z3[pair]
        zs = sigmoid(z)
        mixer = mx3[pair]
        scanned = y3[pair]
        skip = skip_of(pair)
        dy = dgated * (z * zs)
        dz = dgated * (scanned + skip * mixer) * (zs * (1.0 + z * (1.0 - zs)))
        ops_ref[0:length, lanes_of(pair, at_da + 3 * LANES)] = dz.astype(BF)
        put_small(5, lanes_of(pair), row_sum(dy * mixer))
        dyb = dy.astype(BF)
        xt = xt3[pair]
        sides = [jnp.where(left if side == 0 else ~left, dyb, jnp.zeros_like(dyb)) for side in (0, 1)]
        dxt = jnp.zeros((length, LANES), F32)
        for side in range(2):
            head, dys = 2 * pair + side, sides[side]
            top = mm_tn(w4[head, :, 0:half], dys)
            low = mm_tn(w4[head, half:length, half:length], dys[half:length])
            dxt = dxt + jnp.concatenate([top, low], axis=0)
        for bt, bs in ((0, 0), (1, 0), (1, 1)):
            rows = slice(bt * half, (bt + 1) * half)
            cols = slice(bs * half, (bs + 1) * half)
            dgs[rows, cols] += sum(
                mm_nt(sides[side][rows], xt[cols]) * p4[2 * pair + side, rows, cols].astype(F32)
                for side in range(2)
            )
        select = hots[0, pair]
        dcum[...] += mm(halves(dyb.astype(F32) * scanned - xt.astype(F32) * dxt), select)
        ddt[...] += mm(halves(mixer * dxt), select)
        value = f3[pair]
        vs = sigmoid(value)
        df = (dtx3[pair] * dxt + skip * dy) * (vs * (1.0 + value * (1.0 - vs)))
        taps = [tile(hp_ref, k, pair) for k in range(4)]
        dx, tap_terms, offset_term = filter_tile_back(x3[pair], df, taps, masks)
        ops_ref[0:length, lanes_of(pair, at_dx)] = dx.astype(BF)
        for k in range(4):
            put_small(k, lanes_of(pair), tap_terms[k])
        put_small(4, lanes_of(pair), offset_term)
        return carry

    lax.fori_loop(0, pairs, back_pair, 0, unroll=2)

    dgm = jnp.where(allowed, dgs[...], 0.0).astype(BF)
    tangents = [mm_tn(dgm, output_map), mm(dgm, input_map)]
    for part in range(2):
        value = bcf3[part]
        vs = sigmoid(value)
        df = tangents[part] * (vs * (1.0 + value * (1.0 - vs)))
        dv, tap_terms, offset_term = filter_tile_back(bc3[part], df, state_taps(part), masks)
        ops_ref[0:length, at_da + part * LANES : at_da + (part + 1) * LANES] = dv.astype(BF)
        for k in range(4):
            put_small(8 + 2 * k + part, slice(0, LANES), tap_terms[k])
        put_small(16 + part, slice(0, LANES), offset_term)

    dacc = onehot_times(triangle(length, True), dcum[...])
    dstep = (ddt[...] + rate * dacc) * sigmoid(step)
    ops_ref[0:length, at_da + 2 * LANES : at_da + 3 * LANES] = dstep.astype(BF)
    put_small(7, slice(0, LANES), row_sum(dstep))
    put_small(7, slice(LANES, 2 * LANES), row_sum(dt * dacc) * rate)

    dnorm = mm_nt(ops_ref[0:length, at_da:at_dx], wa_ref[...]) + mm_nt(
        ops_ref[0:length, at_dx:at_mixed], wb_ref[:, 0:channels]
    )
    put_small(18, slice(0, width), row_sum(dnorm * (u * inverse)))
    dg = dnorm * gain
    mean = jnp.mean(dg * u, axis=-1, keepdims=True)
    high, low = split(sm_ref[...], 2)
    ops_ref[length : length + SMALL, 0 : sm_ref.shape[1]] = high
    ops_ref[length + SMALL : length + 2 * SMALL, 0 : sm_ref.shape[1]] = low
    du_ref[...] = (inverse * dg - u * (inverse * inverse * inverse * mean)).astype(BF)


def whole_spec(shape):
    return pl.BlockSpec(shape, lambda i, s, n=len(shape): (0,) * n)


def run_layer(
    layer, backward, want_out, index, env, extras_u=(), extras_g=()
):
    inputs, cotangent, segs, hp, blocks, scalars, mine, heads_real = env
    length, width = inputs.shape[2:]
    local = inputs.shape[1]
    channels = hp.shape[-1]
    pairs = channels // LANES
    heads = 2 * pairs
    count = len(blocks) // 4

    def rows_spec():
        return pl.BlockSpec(
            (None, None, length, width),
            lambda i, s: (s[0] * mine + index // local, index % local, 0, 0),
        )

    any_spec = pl.BlockSpec(memory_space=pl.ANY)
    args = [inputs, segs, hp, *extras_u, *blocks]
    in_specs = [
        rows_spec(),
        pl.BlockSpec((None, 1, length), lambda i, s: (s[0] * mine * local + index, 0, 0)),
        pl.BlockSpec((None,) + hp.shape[1:], lambda i, s: (layer, 0, 0)),
    ]
    in_specs += [whole_spec((length, width)) for _ in extras_u]
    in_specs += [any_spec] * len(blocks)
    shapes = []
    if want_out:
        shapes.append(((length, width), BF))
    if extras_u:
        shapes.append(((length, width), BF))
    if backward:
        args += [cotangent, *extras_g]
        in_specs += [rows_spec()] + [whole_spec((length, width)) for _ in extras_g]
        shapes += [
            ((length + 2 * SMALL, 2 * width + 3 * LANES + 3 * channels), BF),
            ((length, width), BF),
        ]
        if extras_g:
            shapes.append(((length, width), BF))
    tiles = (pairs, length, LANES)
    scratch = [
        pltpu.VMEM((width, 3 * LANES + channels), BF),
        pltpu.VMEM((width, 2 * channels), BF),
        pltpu.SemaphoreType.DMA((2, count)),
        pltpu.VMEM((3, length, LANES), F32),
    ]
    scratch += [pltpu.VMEM(tiles, F32) for _ in range(7)]
    scratch += [pltpu.VMEM((2, length, LANES), F32) for _ in range(2)]
    scratch += [
        pltpu.VMEM(tiles, BF),
        pltpu.VMEM((4, pairs, 2 * LANES, LANES), BF),
        pltpu.VMEM((pairs, 3 * LANES, 2 * LANES), BF),
        pltpu.VMEM((8, channels), F32),
        pltpu.VMEM((length, 2 * LANES), BF),
        pltpu.VMEM((length, 2 * LANES), BF),
        pltpu.VMEM((length, 2 * LANES), BF),
        pltpu.VMEM((length, 3 * LANES), BF),
        pltpu.VMEM((LANES, length), F32),
        pltpu.VMEM((length, length), F32),
        pltpu.VMEM((length, LANES), F32),
    ]
    if backward:
        scratch += [
            pltpu.VMEM((heads, length, length), BF),
            pltpu.VMEM(tiles, F32),
            pltpu.VMEM((heads, length, length), BF),
            pltpu.VMEM((length, length), F32),
            pltpu.VMEM((length, LANES), F32),
            pltpu.VMEM((length, LANES), F32),
            pltpu.VMEM((SMALL, max(width, channels)), F32),
        ]
    else:
        scratch.append(pltpu.VMEM((length, channels), BF))
    passes = 3 if backward else 1
    cost = pl.CostEstimate(
        flops=passes * 2 * length * width * (3 * channels + 3 * LANES),
        bytes_accessed=passes * 2 * width * (3 * channels + 3 * LANES),
        transcendentals=passes * heads * length * length,
    )
    plan = (
        backward,
        want_out,
        len(extras_u),
        len(extras_g),
        pairs,
        heads_real,
        count,
    )
    return pl.pallas_call(
        functools.partial(layer_kernel, plan, layer),
        grid_spec=pltpu.PrefetchScalarGridSpec(
            num_scalar_prefetch=1,
            grid=(1,),
            in_specs=in_specs,
            out_specs=[whole_spec(shape) for shape, _ in shapes],
            scratch_shapes=scratch,
        ),
        out_shape=[jax.ShapeDtypeStruct(s, d) for s, d in shapes],
        cost_estimate=cost,
    )(scalars, *args)


def weight_kernel(number, count, heads_real, channels, scalars, *refs):
    refs = list(refs)
    take = lambda size: [refs.pop(0) for _ in range(size)]
    own = [take(number) for _ in range(2)]
    got = [take(number) for _ in range(2)]
    sa_ref, sb_ref, hs_ref, buf, sems = take(5)
    width = sa_ref.shape[0] * sa_ref.shape[1]
    shard = sa_ref.shape[1]
    length = buf.shape[1] - 2 * SMALL

    def copies(layer):
        jobs = []
        for i in range(number):
            jobs.append(pltpu.make_async_copy(own[layer][i], buf.at[i], sems.at[i]))
            jobs.append(
                pltpu.make_async_copy(got[layer][i], buf.at[number + i], sems.at[number + i])
            )
        return jobs

    for layer in range(2):

        @pl.when(scalars[0] == layer)
        def _(layer=layer):
            for job in copies(layer):
                job.start()

    for job in copies(0):
        job.wait()
    at_da = width
    at_dx = width + 3 * LANES + channels
    at_mixed = at_dx + channels
    at_g = at_mixed + channels

    def piece(begin, end):
        return jnp.concatenate([buf[i, 0:length, begin:end] for i in range(2 * number)], axis=0)

    def flipped(begin):
        return jnp.concatenate(
            [
                buf[i, 0:length, begin : begin + width].astype(F32).T.astype(BF)
                for i in range(2 * number)
            ],
            axis=1,
        )

    def put(target, span, value):
        for owner in range(count):
            target[scalars[1 + 2 * count + owner], :, span] = value[
                owner * shard : (owner + 1) * shard
            ].astype(BF)

    wide = max(width, channels)
    totals = sum(
        buf[i, length + k * SMALL : length + (k + 1) * SMALL, 0:wide].astype(F32)
        for i in range(2 * number)
        for k in range(2)
    )
    hs_ref[...] = totals[0:8, 0:channels]
    normed = flipped(0)
    narrow = mm(normed, piece(at_da, at_da + 3 * LANES))
    expand = compact(width, shard, LANES // count, LANES, True)
    states = mm(totals[8:24, 0:LANES].astype(BF), expand)
    row = lax.broadcasted_iota(jnp.int32, (LANES, width), 0)
    sheet = jnp.where(row == heads_real, totals[18:19, 0:width], 0.0)
    for k in range(10):
        sheet = sheet + jnp.where(row == heads_real + 1 + k, states[k : k + 1, :], 0.0)
    put(sa_ref, slice(0, 2 * LANES), narrow[:, 0 : 2 * LANES])
    put(sa_ref, slice(2 * LANES, 3 * LANES), narrow[:, 2 * LANES :] + sheet.T)
    put(sa_ref, slice(3 * LANES, None), mm(normed, piece(at_da + 3 * LANES, at_dx)))
    put(sb_ref, slice(0, channels), mm(normed, piece(at_dx, at_mixed)))
    put(sb_ref, slice(channels, None), mm(flipped(at_g), piece(at_mixed, at_g)))


def run_weights(own, got, scalars, width, channels, heads_real, count):
    number = len(own[0])
    shard = width // count
    length, wide = own[0][0].shape
    args = [*own[0], *own[1], *got[0], *got[1]]
    shapes = [
        ((count, shard, 3 * LANES + channels), BF),
        ((count, shard, 2 * channels), BF),
        ((8, channels), F32),
    ]
    cost = pl.CostEstimate(
        flops=4 * number * length * width * (3 * channels + 3 * LANES),
        bytes_accessed=4 * number * length * wide,
        transcendentals=0,
    )
    return pl.pallas_call(
        functools.partial(weight_kernel, number, count, heads_real, channels),
        grid_spec=pltpu.PrefetchScalarGridSpec(
            num_scalar_prefetch=1,
            grid=(1,),
            in_specs=[pl.BlockSpec(memory_space=pl.ANY)] * len(args),
            out_specs=[whole_spec(shape) for shape, _ in shapes],
            scratch_shapes=[
                pltpu.VMEM((2 * number, length, wide), BF),
                pltpu.SemaphoreType.DMA((2 * number,)),
            ],
        ),
        out_shape=[jax.ShapeDtypeStruct(s, d) for s, d in shapes],
        cost_estimate=cost,
        name="weight_terms",
    )(scalars, *args)


def half_kernel(scalars, *refs):
    for i, ref in enumerate(refs[:-1]):
        refs[-1][i] = ref[...]


def run_half(parts, scalars, share):
    width = parts[0].shape[1]
    last = scalars.shape[0] - 1
    return pl.pallas_call(
        half_kernel,
        grid_spec=pltpu.PrefetchScalarGridSpec(
            num_scalar_prefetch=1,
            grid=(1,),
            in_specs=[pl.BlockSpec((share, width), lambda i, s: (1 - s[last], 0))] * len(parts),
            out_specs=whole_spec((len(parts), share, width)),
        ),
        out_shape=jax.ShapeDtypeStruct((len(parts), share, width), BF),
        name="other_half",
    )(scalars, *parts)


def merge_kernel(number, own, scalars, *refs):
    mids, gmids, parts, (recv_ref, kept_ref, sent_ref) = (
        refs[0:number],
        refs[number : 2 * number],
        refs[2 * number : -3],
        refs[-3:],
    )
    first = scalars[0] == 0
    for group, bases in enumerate((mids, gmids)):
        for i in range(number):
            base = bases[i][...]
            total = base.astype(F32) + recv_ref[group * number + i].astype(F32)
            if own:
                total = total + parts[group * number + i][...].astype(F32)
            total = total.astype(BF)
            zero, one = (base, total) if group == 0 else (total, base)
            kept_ref[group, i] = jnp.where(first, zero, one)
            sent_ref[group, i] = jnp.where(first, one, zero)


def run_merge(mids, gmids, parts, recv, scalars):
    number, share, width = len(mids), recv.shape[1], recv.shape[2]
    last = scalars.shape[0] - 1
    own = len(parts) > 0
    shape = (2, number, share, width)
    return pl.pallas_call(
        functools.partial(merge_kernel, number, own),
        grid_spec=pltpu.PrefetchScalarGridSpec(
            num_scalar_prefetch=1,
            grid=(1,),
            in_specs=[pl.BlockSpec((share, width), lambda i, s: (s[last], 0))]
            * (2 * number + len(parts))
            + [whole_spec(recv.shape)],
            out_specs=[whole_spec(shape)] * 2,
        ),
        out_shape=[jax.ShapeDtypeStruct(shape, BF)] * 2,
        name="merge",
    )(scalars, *mids, *gmids, *parts, recv)


def place_kernel(number, scalars, kept_ref, got_ref, outs_ref, grads_ref):
    mine = scalars[0] * number
    theirs = (1 - scalars[0]) * number
    for group, target in enumerate((outs_ref, grads_ref)):
        target[pl.ds(mine, number)] = kept_ref[group]
        target[pl.ds(theirs, number)] = got_ref[group]


def run_place(kept, got, scalars):
    number = kept.shape[1]
    shape = (2 * number,) + kept.shape[2:]
    return pl.pallas_call(
        functools.partial(place_kernel, number),
        grid_spec=pltpu.PrefetchScalarGridSpec(
            num_scalar_prefetch=1,
            grid=(1,),
            in_specs=[whole_spec(kept.shape)] * 2,
            out_specs=[whole_spec(shape)] * 2,
        ),
        out_shape=[jax.ShapeDtypeStruct(shape, BF)] * 2,
        name="place",
    )(scalars, kept, got)


def pack_kernel(channels_real, state_ref, spare_ref, head_ref, out_ref, *refs):
    wide_refs, line_refs, (a_ref, b_ref, hp_ref) = refs[0:3], refs[3:6], refs[6:]
    hp_ref[...] = jnp.zeros_like(hp_ref)
    begin = 0
    for ref in wide_refs + line_refs:
        hp_ref[begin : begin + ref.shape[0], 0 : ref.shape[1]] = ref[...]
        begin += ref.shape[0]
    shard = state_ref.shape[0]
    channels = b_ref.shape[1] // 2
    a_ref[:, 0 : 2 * LANES] = state_ref[...]
    a_ref[:, 2 * LANES : 3 * LANES] = spare_ref[...]
    row = lax.broadcasted_iota(jnp.int32, (shard, shard), 0)
    col = lax.broadcasted_iota(jnp.int32, (shard, shard), 1)
    identity = jnp.where(row == col, 1.0, 0.0).astype(BF)
    if channels != channels_real:
        a_ref[:, 3 * LANES :] = jnp.zeros((shard, channels), BF)
        b_ref[...] = jnp.zeros_like(b_ref)
    a_ref[:, 3 * LANES : 3 * LANES + channels_real] = head_ref[:, 0, :]
    b_ref[:, 0:channels_real] = head_ref[:, 1, :]
    b_ref[:, channels : channels + channels_real] = mm_nt(identity, out_ref[...]).astype(BF)


def run_pack(state, spare, head, out, wide, lines, channels):
    shard = state.shape[0]
    shapes = [((shard, 3 * LANES + channels), BF), ((shard, 2 * channels), BF), ((9, channels), F32)]
    return pl.pallas_call(
        functools.partial(pack_kernel, head.shape[2]),
        out_shape=[jax.ShapeDtypeStruct(shape, kind) for shape, kind in shapes],
        name="pack",
    )(state, spare, head, out, *wide, *lines)


def ring_order(count):
    return [i for i in range(0, count, 2)] + [i for i in range(1, count, 2)][::-1]


def swap(value, axis):
    return lax.ppermute(value, axis, [(0, 1), (1, 0)])


def device_step(
    inputs,
    segments,
    cotangent,
    norm_gain,
    head_weight,
    step_weight,
    state_weight,
    head_filter,
    head_offset,
    state_filter,
    state_offset,
    step_bias,
    decay_log,
    skip_scale,
    gate_gain,
    output_weight,
):
    sections = lax.axis_size("section")
    count = lax.axis_size("dp")
    tensors = lax.axis_size("tensor")
    section = lax.axis_index("section")
    dp = lax.axis_index("dp")
    tensor = lax.axis_index("tensor")
    first = section == 0
    micros, local, length, width = inputs.shape
    mine = micros // sections
    number = mine * local
    share_rows = length // tensors
    shard = width // count
    channels_real = head_filter.shape[2]
    heads_real = step_bias.shape[1]
    states = state_weight.shape[3]
    pairs = -(-heads_real // 2)
    channels = pairs * LANES

    def pad_last(value, size):
        extra = size - value.shape[-1]
        if extra == 0:
            return value
        return jnp.pad(value, [(0, 0)] * (value.ndim - 1) + [(0, extra)])

    lanes_each = states // count
    tiny = jnp.concatenate([state_filter[0].reshape(8, lanes_each), state_offset[0]], axis=0).T
    tiny = jnp.pad(tiny, ((0, shard - lanes_each), (0, 0)))
    spare = pad_last(
        jnp.concatenate([step_weight[0], norm_gain[0][:, None], tiny], axis=1), LANES
    )
    block_a, block_b, own_params = run_pack(
        state_weight[0].reshape(shard, 2 * states),
        spare,
        head_weight[0],
        output_weight[0],
        (head_filter[0], head_offset, gate_gain),
        (step_bias, decay_log, skip_scale),
        channels,
    )

    order = ring_order(count)
    evens = (count + 1) // 2

    def owner_at(place):
        place = place % count
        return jnp.where(place < evens, 2 * place, 2 * (count - 1 - place) + 1)

    def place_of(owner):
        return jnp.where(owner % 2 == 0, owner // 2, count - 1 - owner // 2)

    position = place_of(dp)
    heading = jnp.where(first, 1, -1)
    hops = []
    for i in range(count):
        hops.append((order[i], order[(i + 1) % count]))
        hops.append((count + order[i], count + order[(i - 1) % count]))

    def around(value):
        return lax.ppermute(value, ("section", "dp"), hops)

    def gather(block):
        own, other = [], []
        current = block
        for hop in range(count):
            if hop:
                current = around(current)
            own.append(current)
            other.append(swap(current, "section"))
        return own + other

    blocks = gather(block_a) + gather(block_b)
    index = jnp.arange(2 + 3 * count) - 1
    hop_index = index % count
    turned = jnp.where(index < count, -heading, heading) * hop_index
    ring_slot = ((position - place_of(hop_index)) * heading - 1) % count
    scalars = jnp.where(index < 2 * count, owner_at(position + turned), ring_slot)
    scalars = jnp.where(index < 0, section, scalars)
    scalars = jnp.where(index == 3 * count, tensor, scalars).astype(jnp.int32)

    other_params = swap(own_params, "section")
    hp = jnp.stack(
        [
            jnp.where(first, own_params, other_params),
            jnp.where(first, other_params, own_params),
        ]
    )

    segs = segments.reshape(micros * local, 1, length).astype(F32)
    env = (inputs, cotangent, segs, hp, blocks, scalars, mine, heads_real)

    def pieces(partial):
        if tensors == 2:
            return (partial, swap(partial, "tensor"))
        return (lax.psum(partial.astype(F32), "tensor"),)

    to_one = lambda value: lax.ppermute(value, "section", [(0, 1)])
    to_zero = lambda value: lax.ppermute(value, "section", [(1, 0)])

    fronts = [pieces(run_layer(0, False, True, i, env)[0]) for i in range(number)]
    middle, outs, backs, ops_one, got_one = [], [], [], [], []
    for i in range(number):
        partial, rows, ops, back = run_layer(1, True, True, i, env, extras_u=fronts[i])
        middle.append(rows)
        backs.append(pieces(back))
        outs.append(partial)
        ops_one.append(ops)
        got_one.append(to_one(ops))
    ops_zero, got_zero, front_backs, mid_grads = [], [], [], []
    for i in range(number):
        ops, back, rows = run_layer(0, True, False, i, env, extras_g=backs[i])
        ops_zero.append(ops)
        mid_grads.append(rows)
        got_zero.append(to_zero(ops))
        front_backs.append(back)

    parts = outs + front_backs
    if tensors == 2:
        recv = swap(run_half(parts, scalars, share_rows), "tensor")
    else:
        recv = jnp.stack(
            [
                lax.psum_scatter(part.astype(F32), "tensor", scatter_dimension=0, tiled=True)
                for part in parts
            ]
        )
        parts = []

    sums_a, sums_b, head_small = run_weights(
        (ops_zero, ops_one),
        (got_zero, got_one),
        scalars,
        width,
        channels,
        heads_real,
        count,
    )

    heads_total = head_small
    doubling = count & (count - 1) == 0
    if not doubling:
        heads_total = lax.psum(heads_total, "dp")
    sent = kept = got = outputs = input_grads = None
    total_a, total_b = sums_a[0], sums_b[0]
    bit = 1
    for hop in range(1, count):
        total_a = around(total_a)
        total_b = around(total_b)
        total_a = total_a.astype(F32) + sums_a[hop].astype(F32)
        total_b = total_b.astype(F32) + sums_b[hop].astype(F32)
        if hop < count - 1:
            total_a, total_b = total_a.astype(BF), total_b.astype(BF)
        if hop >= 2 and bit < count and doubling:
            total_b, heads_total = lax.optimization_barrier((total_b, heads_total))
            heads_total = heads_total + lax.ppermute(
                heads_total, "dp", [(i, i ^ bit) for i in range(count)]
            )
            bit *= 2
        if hop == 1:
            total_a, recv = lax.optimization_barrier((total_a, recv))
            kept, sent = run_merge(middle, mid_grads, parts, recv, scalars)
            got = swap(sent, "section")
        if hop == min(5, count - 1):
            total_a, got = lax.optimization_barrier((total_a, got))
            outputs, input_grads = run_place(kept, got, scalars)
    shape_out = (1, micros, local, share_rows, width)
    outputs, input_grads = outputs.reshape(shape_out), input_grads.reshape(shape_out)
    shared = total_a[:, : 2 * states + LANES]
    if tensors == 2:
        shared_sum = shared + swap(shared.astype(BF), "tensor").astype(F32)
    else:
        shared_sum = lax.psum(shared.astype(BF), "tensor").astype(F32)
    state_grad = shared_sum[:, : 2 * states].reshape(shard, 2, states)
    step_grad = shared[:, 2 * states : 2 * states + heads_real]
    spare_sum = shared_sum[:, 2 * states + heads_real :]
    gain_grad = spare_sum[:, 0]
    tiny_sum = spare_sum[:lanes_each, 1:11].T
    filter_grad = tiny_sum[0:8].reshape(4, 2, lanes_each)
    offset_grad = tiny_sum[8:10]
    head_grad = jnp.stack(
        [total_a[:, 2 * states + LANES :][:, :channels_real], total_b[:, :channels_real]], axis=1
    )
    output_grad = total_b[:, channels : channels + channels_real].T

    skip_grad = heads_total[5].reshape(-1, HEADDIM).sum(axis=1)[:heads_real]

    return (
        outputs,
        input_grads,
        gain_grad[None],
        head_grad[None],
        step_grad[None],
        state_grad[None],
        heads_total[None, 0:4, :channels_real],
        heads_total[None, 4, :channels_real],
        filter_grad[None],
        offset_grad[None],
        heads_total[None, 7, 0:heads_real],
        heads_total[None, 7, LANES : LANES + heads_real],
        skip_grad[None],
        heads_total[None, 6, :channels_real],
        output_grad[None],
    )


def solution(mesh):
    placed = (
        P(None, "dp", None, None),
        P(None, "dp", None),
        P(None, "dp", None, None),
        P("section", "dp"),
        P("section", "dp", None, "tensor"),
        P("section", "dp", "tensor"),
        P("section", "dp", None, None),
        P("section", None, "tensor"),
        P("section", "tensor"),
        P("section", None, None, "dp"),
        P("section", None, "dp"),
        P("section", "tensor"),
        P("section", "tensor"),
        P("section", "tensor"),
        P("section", "tensor"),
        P("section", "tensor", "dp"),
    )
    return jax.shard_map(
        device_step,
        mesh=mesh,
        in_specs=placed,
        out_specs=(
            P("section", None, "dp", "tensor", None),
            P("section", None, "dp", "tensor", None),
            P("section", "dp"),
            P("section", "dp", None, "tensor"),
            P("section", "dp", "tensor"),
            P("section", "dp", None, None),
            P("section", None, "tensor"),
            P("section", "tensor"),
            P("section", None, None, "dp"),
            P("section", None, "dp"),
            P("section", "tensor"),
            P("section", "tensor"),
            P("section", "tensor"),
            P("section", "tensor"),
            P("section", "tensor", "dp"),
        ),
        check_vma=False,
    )
```
